32 devices in a mesh: seq: 8 (over z, x), head: 4 (over y, core).
Axes of the slice: x: 2, y: 2, z: 4, core: 2. Of those that a mesh axis runs over, the one named last changes fastest.
Arguments:
- queries: bfloat16 [2, 4096, 4096], P(None, ('seq', 'head')), may hold values from -6 to 6
- memory_keys: bfloat16 [2, 4096, 4096], P(None, ('seq', 'head')), may hold values from -6 to 6
- memory_values: bfloat16 [2, 4096, 4096], P(None, ('seq', 'head')), may hold values from -6 to 6
- rates: float32 [2, 4096, 8], P(None, ('seq', 'head')), may hold values from 0.001 to 0.01
- fast_gate: float32 [8, 512, 512], P('head'), may hold values from -0.25 to 0.25
- fast_up: float32 [8, 512, 512], P('head'), may hold values from -0.25 to 0.25
- fast_down: float32 [8, 512, 512], P('head'), may hold values from -0.25 to 0.25
Outputs:
- outputs: bfloat16 [2, 4096, 4096], P(None, ('seq', 'head'))
- final_gate: float32 [8, 512, 512], P('head')
- final_up: float32 [8, 512, 512], P('head')
- final_down: float32 [8, 512, 512], P('head')
The draws below stay inside these ranges and needn't reach their ends.
All inputs are finite; a program needn't handle non-finite values.
Results may differ from the reference program's by a relative error of at most 0.035.
Values may be sent and summed in bfloat16 or wider, within the bound.
No kernel may reach another device: no remote copies, remote signals or barrier semaphores. Data moves between devices by JAX's collectives and lax.ppermute only.
A program may use at most 128 MiB of HBM per device.

```python
import math
import jax
import jax.numpy as jnp
from jax import lax

HEADS = 8
HD = 512
FH = 512
SPANS = 2
D = 4096
TOKENS = 4096


def steps_of(own_key, dims, split, low, high):
    loudness = 1.0
    for axis_at, shards_of in split:
        draws = jax.random.uniform(jax.random.fold_in(jax.random.fold_in(own_key, 6), axis_at), (shards_of,), jnp.float32, low / len(split), high / len(split))
        loudness = loudness * jnp.repeat(jnp.exp(draws), dims[axis_at] // shards_of).reshape((-1,) + (1,) * (len(dims) - 1 - axis_at))
    return loudness


def normal_values(stream_key, extent, deviation, limit, split=(), kind=jnp.bfloat16):
    entries = jax.random.normal(stream_key, extent, jnp.float32) * deviation
    if len(split) > 0:
        entries = steps_of(stream_key, extent, split, -0.22, 0.18) * entries
    return jnp.clip(entries, min=-limit, max=limit).astype(kind)


def setup_inputs(seed: int = 0) -> dict:
    key_of = jax.random.split(jax.random.key(seed), 8)
    queries = normal_values(key_of[0], (SPANS, TOKENS, D), 1.0, 6.0, ((1, 32),))
    memory_keys = normal_values(key_of[1], (SPANS, TOKENS, D), 1.0, 6.0, ((1, 32),))
    memory_values = normal_values(key_of[2], (SPANS, TOKENS, D), 1.0, 6.0, ((1, 32),))
    rates = jnp.clip(jnp.exp(math.log(0.01) - 2.30258502 * jax.random.uniform(key_of[3], (SPANS, TOKENS, HEADS), jnp.float32) ** steps_of(key_of[3], (SPANS, TOKENS, HEADS), ((1, 32),), -0.2, 0.2)), 0.001, 0.01)
    fast_gate = normal_values(key_of[4], (HEADS, HD, FH), HD ** -0.5, 0.25, ((0, 4),), jnp.float32)
    fast_up = normal_values(key_of[5], (HEADS, HD, FH), HD ** -0.5, 0.25, ((0, 4),), jnp.float32)
    fast_down = normal_values(key_of[6], (HEADS, FH, HD), FH ** -0.5, 0.25, ((0, 4),), jnp.float32)
    return {"queries": queries, "memory_keys": memory_keys, "memory_values": memory_values, "rates": rates, "fast_gate": fast_gate, "fast_up": fast_up, "fast_down": fast_down}


EPSILON = 1e-06

def head_gradients(gate_weight, up_weight, down_weight, key_block, value_block, rate_block):
    gate_half = gate_weight.astype(jnp.bfloat16)
    up_half = up_weight.astype(jnp.bfloat16)
    down_half = down_weight.astype(jnp.bfloat16)
    gate_pre = jnp.dot(key_block, gate_half, preferred_element_type=jnp.float32)
    up_pre = jnp.dot(key_block, up_half, preferred_element_type=jnp.float32)
    sigmoid_gate = jax.nn.sigmoid(gate_pre)
    activated = gate_pre * sigmoid_gate
    hidden = (activated * up_pre).astype(jnp.bfloat16)
    target = (-rate_block[:, None] * value_block.astype(jnp.float32)).astype(jnp.bfloat16)
    grad_down = jnp.dot(hidden.T, target, preferred_element_type=jnp.float32)
    hidden_grad = jnp.dot(target, down_half.T, preferred_element_type=jnp.float32)
    gate_delta = (hidden_grad * up_pre * sigmoid_gate * (1.0 + gate_pre * (1.0 - sigmoid_gate))).astype(jnp.bfloat16)
    up_delta = (hidden_grad * activated).astype(jnp.bfloat16)
    grad_gate = jnp.dot(key_block.T, gate_delta, preferred_element_type=jnp.float32)
    grad_up = jnp.dot(key_block.T, up_delta, preferred_element_type=jnp.float32)
    return (grad_gate, grad_up, grad_down)

def renormalize(weight, gradient):
    updated = weight - gradient
    old_norm = jnp.sqrt(lax.optimization_barrier(jnp.sum(weight * weight, axis=-2, keepdims=True)) + EPSILON)
    new_norm = jnp.sqrt(lax.optimization_barrier(jnp.sum(updated * updated, axis=-2, keepdims=True)) + EPSILON)
    return updated * (old_norm / new_norm)

def apply_head(gate_weight, up_weight, down_weight, query_block):
    gate_pre = jnp.dot(query_block, gate_weight.astype(jnp.bfloat16), preferred_element_type=jnp.float32)
    up_pre = jnp.dot(query_block, up_weight.astype(jnp.bfloat16), preferred_element_type=jnp.float32)
    hidden = (jax.nn.silu(gate_pre) * up_pre).astype(jnp.bfloat16)
    return jnp.dot(hidden, down_weight.astype(jnp.bfloat16), preferred_element_type=jnp.float32).astype(jnp.bfloat16)

def reference(queries, memory_keys, memory_values, rates, fast_gate, fast_up, fast_down):
    gate_state, up_state, down_state = (fast_gate, fast_up, fast_down)
    results = []
    for block_index in range(SPANS):
        key_heads = memory_keys[block_index].reshape(TOKENS, HEADS, HD)
        value_heads = memory_values[block_index].reshape(TOKENS, HEADS, HD)
        query_heads = queries[block_index].reshape(TOKENS, HEADS, HD)
        grad_gate, grad_up, grad_down = jax.vmap(head_gradients, in_axes=(0, 0, 0, 1, 1, 1))(gate_state, up_state, down_state, key_heads, value_heads, rates[block_index])
        gate_state = renormalize(gate_state, grad_gate)
        up_state = renormalize(up_state, grad_up)
        down_state = renormalize(down_state, grad_down)
        applied = jax.vmap(apply_head, in_axes=(0, 0, 0, 1), out_axes=1)(gate_state, up_state, down_state, query_heads)
        results.append(applied.reshape(TOKENS, D))
    return (jnp.stack(results), gate_state, up_state, down_state)
```

```python
import jax
import jax.numpy as jnp
from jax import lax
from jax.sharding import Mesh, PartitionSpec as P

EPSILON = 1e-06
AXES = ("outer", "inner", "pair", "core")
GROUP = ("pair", "inner", "core")


def gradients(weights, keys, target):
    gate_half, up_half, down_half = (weights[0], weights[1], weights[2])
    gate_pre = jnp.dot(keys, gate_half, preferred_element_type=jnp.float32)
    up_pre = jnp.dot(keys, up_half, preferred_element_type=jnp.float32)
    sigmoid_gate = jax.nn.sigmoid(gate_pre)
    activated = gate_pre * sigmoid_gate
    hidden = (activated * up_pre).astype(jnp.bfloat16)
    hidden_grad = jnp.dot(target, down_half.T, preferred_element_type=jnp.float32)
    gate_delta = (
        hidden_grad * up_pre * sigmoid_gate * (1.0 + gate_pre * (1.0 - sigmoid_gate))
    ).astype(jnp.bfloat16)
    up_delta = (hidden_grad * activated).astype(jnp.bfloat16)
    return jnp.stack(
        [
            jnp.dot(keys.T, gate_delta, preferred_element_type=jnp.float32),
            jnp.dot(keys.T, up_delta, preferred_element_type=jnp.float32),
            jnp.dot(hidden.T, target, preferred_element_type=jnp.float32),
        ]
    )


def renormalize(weight, gradient):
    updated = weight - gradient
    old_norm = jnp.sqrt(jnp.sum(weight * weight, axis=-2, keepdims=True) + EPSILON)
    new_norm = jnp.sqrt(jnp.sum(updated * updated, axis=-2, keepdims=True) + EPSILON)
    return updated * (old_norm / new_norm)


def apply_head(weights, query):
    gate_pre = jnp.dot(query, weights[0], preferred_element_type=jnp.float32)
    up_pre = jnp.dot(query, weights[1], preferred_element_type=jnp.float32)
    hidden = (jax.nn.silu(gate_pre) * up_pre).astype(jnp.bfloat16)
    return jnp.dot(hidden, weights[2], preferred_element_type=jnp.float32).astype(jnp.bfloat16)


def solution(mesh):
    seq, head = (mesh.shape["seq"], mesh.shape["head"])

    def whole(queries, memory_keys, memory_values, rates, fast_gate, fast_up, fast_down):
        heads, head_size = (fast_gate.shape[0], fast_gate.shape[1])
        spans, tokens, width = queries.shape
        local = heads // head
        inner = 2 * local
        outer = seq // inner
        pair = head // 2
        fine = Mesh(mesh.devices.reshape(outer, inner, pair, 2), AXES)
        places = [
            (o, i, p, c)
            for o in range(outer)
            for i in range(inner)
            for p in range(pair)
            for c in range(2)
        ]
        number = {place: n for n, place in enumerate(places)}

        def permute(value, source_of):
            links = []
            for place in places:
                source = source_of(*place)
                if source is not None:
                    links.append((number[source], number[place]))
            return lax.ppermute(value, AXES, links)

        def other_core(value):
            return permute(value, lambda o, i, p, c: (o, i, p, 1 - c))

        def across(value):
            if outer == 2:
                return value.astype(jnp.float32) + permute(
                    value, lambda o, i, p, c: (1 - o, i, p, c)
                ).astype(jnp.float32)
            return lax.psum(value.astype(jnp.float32), "outer")

        def on_device(queries, memory_keys, memory_values, rates, *fast):
            core = lax.axis_index("core")
            chip = lax.axis_index("inner")
            rows = queries.shape[1]
            half = head_size // 2

            def to_heads(value):
                blocks = value.reshape(2, rows // 2, heads, head_size).transpose(2, 0, 1, 3)
                blocks = blocks.reshape(heads * 2, rows // 2, head_size)
                got = lax.all_to_all(blocks, GROUP, 0, 0, tiled=True)
                return got.reshape(heads * rows, head_size)

            def to_tokens(value):
                blocks = value.reshape(heads * 2, rows // 2, head_size)
                got = lax.all_to_all(blocks, GROUP, 0, 0, tiled=True)
                got = got.reshape(heads, 2, rows // 2, head_size).transpose(1, 2, 0, 3)
                return got.reshape(rows, width)

            scaled = (
                -rates[..., None]
                * memory_values.reshape(spans, rows, heads, head_size).astype(jnp.float32)
            ).astype(jnp.bfloat16).reshape(spans, rows, width)
            mine = jnp.stack(
                [lax.dynamic_index_in_dim(one, chip % local, 0, False) for one in fast]
            )
            sent = permute(
                mine, lambda o, i, p, c: (o, i, p, i // local) if c != i // local else None
            )
            full = jnp.where(core == chip // local, mine, sent)
            state = lax.dynamic_slice_in_dim(full, core * half, half, 2)
            weights = full.astype(jnp.bfloat16)
            results = []
            for span in range(spans):
                keys = to_heads(memory_keys[span])
                target = to_heads(scaled[span])
                grads = gradients(weights, keys, target)
                keep = lax.dynamic_slice_in_dim(grads, core * half, half, 2)
                give = lax.dynamic_slice_in_dim(grads, (1 - core) * half, half, 2)
                partial = keep + other_core(give.astype(jnp.bfloat16)).astype(jnp.float32)
                state = renormalize(state, across(partial.astype(jnp.bfloat16)))
                own = state.astype(jnp.bfloat16)
                rest = other_core(own)
                weights = jnp.where(
                    core == 0,
                    jnp.concatenate([own, rest], 2),
                    jnp.concatenate([rest, own], 2),
                )
                results.append(to_tokens(apply_head(weights, to_heads(queries[span]))))
            shifted = []
            for shift in range(local):
                near = weights
                if shift:
                    near = permute(
                        weights,
                        lambda o, i, p, c: (
                            (o, c * local + (i + shift) % local, p, c) if c == i // local else None
                        ),
                    )
                far = permute(
                    weights,
                    lambda o, i, p, c: (
                        (o, c * local + (i + shift) % local, p, c) if c != i // local else None
                    ),
                )
                shifted.append(jnp.where(core == chip // local, near, far))
            slots = []
            for slot in range(local):
                chosen = shifted[0]
                for shift in range(1, local):
                    chosen = jnp.where((chip + shift) % local == slot, shifted[shift], chosen)
                slots.append(chosen)
            final = [
                jnp.stack([slot[matrix] for slot in slots]).astype(jnp.float32)
                for matrix in range(3)
            ]
            return (jnp.stack(results), *final)

        by_token = P(None, AXES, None)
        by_head = P(("pair", "core"), None, None)
        return jax.shard_map(
            on_device,
            mesh=fine,
            in_specs=(by_token,) * 4 + (by_head,) * 3,
            out_specs=(by_token,) + (by_head,) * 3,
            check_vma=False,
        )(queries, memory_keys, memory_values, rates, fast_gate, fast_up, fast_down)

    return whole
```

```python
import jax
import jax.numpy as jnp
from jax import lax
from jax.experimental import pallas as pl
from jax.experimental.pallas import tpu as pltpu
from jax.sharding import Mesh, PartitionSpec as P

EPSILON = 1e-06
AXES = ("outer", "inner", "pair", "core")
GROUP = ("pair", "inner", "core")


def room(mebibytes):
    return pltpu.CompilerParams(vmem_limit_bytes=mebibytes * 1024 * 1024)


BF16 = jnp.bfloat16
F32 = jnp.float32


def dot(left, right, dims):
    return lax.dot_general(left, right, ((dims[:1], dims[1:]), ((), ())), preferred_element_type=F32)


def pack_rated(span, keys, values, rates_by_head, steps=2):
    _, rows, width = keys.shape
    heads = rates_by_head.shape[1]
    size, part = (width // heads, rows // 2)
    each = part // steps

    def body(key_ref, value_ref, rate_ref, out_ref, column_ref):
        at = pl.program_id(0) * steps + pl.program_id(1)

        @pl.when(at == 0)
        def _():
            column_ref[...] = rate_ref[0].T

        rate = column_ref[pl.ds(pl.multiple_of(at * each, each), each)]
        for h in range(heads):
            columns = slice(h * size, (h + 1) * size)
            out_ref[h, 0, 0] = key_ref[0, :, columns]
            scale = -rate[:, h : h + 1]
            out_ref[h, 0, 1] = (scale * value_ref[0, :, columns].astype(F32)).astype(BF16)

    block = pl.BlockSpec((1, each, width), lambda w, n: (span, w * steps + n, 0))
    packed = pl.pallas_call(
        body,
        grid=(2, steps),
        in_specs=[block, block, pl.BlockSpec((1, heads, rows), lambda w, n: (span, 0, 0))],
        out_specs=pl.BlockSpec((heads, 1, 2, each, size), lambda w, n: (0, w, 0, n, 0)),
        out_shape=jax.ShapeDtypeStruct((heads, 2, 2, part, size), BF16),
        scratch_shapes=[pltpu.VMEM((rows, heads), F32)],
        compiler_params=room(8),
        name="pack_rated",
    )(keys, values, rates_by_head)
    return packed.reshape(heads * 2, rows, size)


def pack_spans(value, heads, steps=2):
    spans, rows, width = value.shape
    size, part = (width // heads, rows // 2)
    each = part // steps

    def body(in_ref, out_ref):
        for h in range(heads):
            out_ref[h, 0] = in_ref[:, :, h * size : (h + 1) * size]

    packed = pl.pallas_call(
        body,
        grid=(2, steps),
        in_specs=[pl.BlockSpec((spans, each, width), lambda w, n: (0, w * steps + n, 0))],
        out_specs=pl.BlockSpec((heads, 1, spans, each, size), lambda w, n: (0, w, 0, n, 0)),
        out_shape=jax.ShapeDtypeStruct((heads, 2, spans, part, size), BF16),
        compiler_params=room(8),
        name="pack_spans",
    )(value)
    return packed.reshape(heads * 2, spans * part, size)


def unpack(got, span, spans, before, steps=2):
    count, part, size = got.shape
    heads, rows = (count // 2, 2 * part)
    each = part // steps

    def body(in_ref, *refs):
        for h in range(heads):
            refs[-1][0, :, h * size : (h + 1) * size] = in_ref[h, 0]

    kept = [] if before is None else [before]
    return pl.pallas_call(
        body,
        grid=(2, steps),
        in_specs=[pl.BlockSpec((heads, 1, each, size), lambda w, n: (0, w, n, 0))]
        + [pl.BlockSpec(memory_space=pl.ANY) for _ in kept],
        out_specs=pl.BlockSpec((1, each, heads * size), lambda w, n: (span, w * steps + n, 0)),
        out_shape=jax.ShapeDtypeStruct((spans, rows, heads * size), BF16),
        input_output_aliases={1: 0} if kept else {},
        compiler_params=room(6),
        name="unpack",
    )(got.reshape(heads, 2, part, size), *kept)


def start_state(place, sent, fast):
    _, size, hidden = fast[0].shape
    half = hidden // 2

    def body(place_ref, *refs):
        for core in range(2):
            @pl.when(place_ref[0] == core)
            def _():
                for matrix in range(3):
                    full = jnp.where(place_ref[2] == 1, refs[3 + matrix][0], refs[matrix][...])
                    own = full[:, core * half : (core + 1) * half]
                    rest = full[:, (1 - core) * half : (2 - core) * half]
                    refs[6 + matrix][...] = own
                    refs[9 + matrix][...] = own.astype(BF16)
                    refs[12 + matrix][...] = rest.astype(BF16)

    spec = pltpu.PrefetchScalarGridSpec(
        num_scalar_prefetch=1,
        grid=(1,),
        in_specs=[pl.BlockSpec((size, hidden), lambda n, place: (0, 0))] * 3
        + [pl.BlockSpec((1, size, hidden), lambda n, place: (place[1], 0, 0))] * 3,
        out_specs=[pl.BlockSpec((size, half), lambda n, place: (0, 0))] * 9,
    )
    made = pl.pallas_call(
        body,
        grid_spec=spec,
        out_shape=[jax.ShapeDtypeStruct((size, half), F32)] * 3
        + [jax.ShapeDtypeStruct((size, half), BF16)] * 6,
        compiler_params=room(32),
        name="start_state",
    )(place, *sent, *fast)
    return (list(made[:3]), list(made[3:6]), list(made[6:]))


def join_halves(place_ref, own_refs, rest_refs, full_refs):
    half = own_refs[0].shape[-1]
    for core in range(2):
        @pl.when(place_ref[0] == core)
        def _():
            for own_ref, rest_ref, full_ref in zip(own_refs, rest_refs, full_refs):
                full_ref[:, core * half : (core + 1) * half] = own_ref[...]
                full_ref[:, (1 - core) * half : (2 - core) * half] = rest_ref[...]


def gradients(place, own, rest, got, steps=4):
    sources, rows, size = got.shape
    half = own[0].shape[-1]
    hidden_size, part = (2 * half, rows // 2)
    each = sources // steps

    def body(place_ref, *refs):
        got_ref, keep_refs, give_refs = (refs[6], refs[7:10], refs[10:13])
        full_refs, sum_refs = (refs[13:16], refs[16:19])
        step = pl.program_id(0)

        @pl.when(step == 0)
        def _():
            join_halves(place_ref, refs[:3], refs[3:6], full_refs)
            for sum_ref in sum_refs:
                sum_ref[...] = jnp.zeros_like(sum_ref)

        keys = got_ref[:, :part].reshape(each * part, size)
        target = got_ref[:, part:].reshape(each * part, size)
        gate_pre = dot(keys, full_refs[0][...], (1, 0))
        up_pre = dot(keys, full_refs[1][...], (1, 0))
        hidden_grad = dot(target, full_refs[2][...], (1, 1))
        sigmoid_gate = jax.nn.sigmoid(gate_pre)
        activated = gate_pre * sigmoid_gate
        hidden = (activated * up_pre).astype(BF16)
        gate_delta = (
            hidden_grad * up_pre * sigmoid_gate * (1.0 + gate_pre * (1.0 - sigmoid_gate))
        ).astype(BF16)
        up_delta = (hidden_grad * activated).astype(BF16)
        sum_refs[0][...] += dot(keys, gate_delta, (0, 0))
        sum_refs[1][...] += dot(keys, up_delta, (0, 0))
        sum_refs[2][...] += dot(hidden, target, (0, 0))

        @pl.when(step == steps - 1)
        def _():
            for core in range(2):
                @pl.when(place_ref[0] == core)
                def _():
                    for keep_ref, give_ref, sum_ref in zip(keep_refs, give_refs, sum_refs):
                        keep_ref[...] = sum_ref[:, core * half : (core + 1) * half]
                        give = sum_ref[:, (1 - core) * half : (2 - core) * half]
                        give_ref[...] = give.astype(BF16)

    flat = lambda n, place: (0, 0)
    spec = pltpu.PrefetchScalarGridSpec(
        num_scalar_prefetch=1,
        grid=(steps,),
        in_specs=[pl.BlockSpec((size, half), flat)] * 6
        + [pl.BlockSpec((each, rows, size), lambda n, place: (n, 0, 0))],
        out_specs=[pl.BlockSpec((size, half), flat)] * 6,
        scratch_shapes=[pltpu.VMEM((size, hidden_size), BF16)] * 3
        + [pltpu.VMEM((size, hidden_size), F32)] * 3,
    )
    made = pl.pallas_call(
        body,
        grid_spec=spec,
        out_shape=[jax.ShapeDtypeStruct((size, half), F32)] * 3
        + [jax.ShapeDtypeStruct((size, half), BF16)] * 3,
        compiler_params=room(24),
        name="gradients",
    )(place, *own, *rest, got)
    return (made[:3], made[3:])


def combine(keep, received):
    def body(keep_ref, received_ref, out_ref):
        out_ref[...] = (keep_ref[...] + received_ref[...].astype(F32)).astype(BF16)

    return pl.pallas_call(
        body, out_shape=jax.ShapeDtypeStruct(keep.shape, BF16), compiler_params=room(4), name="combine"
    )(keep, received)


def update(state, mine, theirs):
    def body(state_ref, mine_ref, theirs_ref, new_ref, half_ref):
        weight = state_ref[...]
        updated = weight - (mine_ref[...].astype(F32) + theirs_ref[...].astype(F32))
        old_norm = jnp.sqrt(jnp.sum(weight * weight, axis=0, keepdims=True) + EPSILON)
        new_norm = jnp.sqrt(jnp.sum(updated * updated, axis=0, keepdims=True) + EPSILON)
        new = updated * (old_norm / new_norm)
        new_ref[...] = new
        half_ref[...] = new.astype(BF16)

    return pl.pallas_call(
        body,
        out_shape=[
            jax.ShapeDtypeStruct(state.shape, F32),
            jax.ShapeDtypeStruct(state.shape, BF16),
        ],
        compiler_params=room(8),
        name="update",
    )(state, mine, theirs)


def applied(place, own, rest, got, span, spans, steps=4):
    sources, rows, size = got.shape
    half, part = (own[0].shape[-1], rows // spans)
    each = sources // steps

    def body(place_ref, *refs):
        got_ref, out_ref, full_refs = (refs[6], refs[7], refs[8:])

        @pl.when(pl.program_id(0) == 0)
        def _():
            join_halves(place_ref, refs[:3], refs[3:6], full_refs)

        query = got_ref[...].reshape(each * part, size)
        gate_pre = dot(query, full_refs[0][...], (1, 0))
        up_pre = dot(query, full_refs[1][...], (1, 0))
        hidden = (gate_pre * jax.nn.sigmoid(gate_pre) * up_pre).astype(BF16)
        result = dot(hidden, full_refs[2][...], (1, 0)).astype(BF16)
        out_ref[...] = result.reshape(each, part, size)

    spec = pltpu.PrefetchScalarGridSpec(
        num_scalar_prefetch=1,
        grid=(steps,),
        in_specs=[pl.BlockSpec((size, half), lambda n, place: (0, 0))] * 6
        + [pl.BlockSpec((each, part, size), lambda n, place: (n, span, 0))],
        out_specs=pl.BlockSpec((each, part, size), lambda n, place: (n, 0, 0)),
        scratch_shapes=[pltpu.VMEM((size, 2 * half), BF16)] * 3,
    )
    return pl.pallas_call(
        body,
        grid_spec=spec,
        out_shape=jax.ShapeDtypeStruct((sources, part, size), BF16),
        compiler_params=room(16),
        name="applied",
    )(place, *own, *rest, got)


def joined(place, own, rest):
    size, half = own.shape

    def body(place_ref, own_ref, rest_ref, full_ref):
        join_halves(place_ref, [own_ref], [rest_ref], [full_ref])

    spec = pltpu.PrefetchScalarGridSpec(
        num_scalar_prefetch=1,
        grid=(1,),
        in_specs=[pl.BlockSpec((size, half), lambda n, place: (0, 0))] * 2,
        out_specs=pl.BlockSpec((size, 2 * half), lambda n, place: (0, 0)),
    )
    return pl.pallas_call(
        body,
        grid_spec=spec,
        out_shape=jax.ShapeDtypeStruct((size, 2 * half), BF16),
        compiler_params=room(4),
        name="joined",
    )(place, own, rest)


def final_state(place, full, near, far):
    count = 1 + len(near)
    size, hidden = full.shape

    def body(place_ref, *refs):
        near_refs, far_refs, out_ref = (refs[:count], refs[count:-1], refs[-1])
        for shift in range(count):
            for home in range(2):
                at = near_refs[shift]
                if home == 0:
                    at = far_refs[shift - 1] if shift else near_refs[1]

                @pl.when((pl.program_id(0) == shift) & (place_ref[2] == home))
                def _():
                    out_ref[0] = at[...].astype(F32)

    spec = pltpu.PrefetchScalarGridSpec(
        num_scalar_prefetch=1,
        grid=(count,),
        in_specs=[pl.BlockSpec((size, hidden), lambda n, place: (0, 0))] * (2 * count - 1),
        out_specs=pl.BlockSpec(
            (1, size, hidden), lambda n, place: (lax.rem(place[1] + n, count), 0, 0)
        ),
    )
    return pl.pallas_call(
        body,
        grid_spec=spec,
        out_shape=jax.ShapeDtypeStruct((count, size, hidden), F32),
        compiler_params=room(10),
        name="final_state",
    )(place, full, *near, *far)


ORDER = (2, 0, 1)


def solution(mesh):
    seq, head = (mesh.shape["seq"], mesh.shape["head"])

    def whole(queries, memory_keys, memory_values, rates, fast_gate, fast_up, fast_down):
        heads = fast_gate.shape[0]
        spans = queries.shape[0]
        local = heads // head
        inner = 2 * local
        outer = seq // inner
        pair = head // 2
        fine = Mesh(mesh.devices.reshape(outer, inner, pair, 2), AXES)
        places = [
            (o, i, p, c)
            for o in range(outer)
            for i in range(inner)
            for p in range(pair)
            for c in range(2)
        ]
        number = {place: n for n, place in enumerate(places)}

        def permute(value, source_of):
            links = []
            for place in places:
                source = source_of(*place)
                if source is not None:
                    links.append((number[source], number[place]))
            return lax.ppermute(value, AXES, links)

        def other_core(value):
            return permute(value, lambda o, i, p, c: (o, i, p, 1 - c))

        def across(value):
            if outer == 2:
                return permute(value, lambda o, i, p, c: (1 - o, i, p, c))
            return lax.psum(value.astype(F32), "outer") - value.astype(F32)

        def nearest(value, shift):
            def source(o, i, p, c):
                if c == i // local:
                    return (o, c * local + (i + shift) % local, p, c)
                return (o, c * local + i % local, p, 1 - c) if shift == 1 else None

            return permute(value, source)

        def onward(value, shift, along):
            def source(o, i, p, c):
                if c == i // local:
                    return None
                if along:
                    return (o, i // local * local + (i + shift) % local, p, c)
                return (o, c * local + i % local, p, c)

            return permute(value, source)

        def exchange(blocks):
            return lax.all_to_all(blocks, GROUP, 0, 0, tiled=True)

        def on_device(queries, memory_keys, memory_values, rates, *fast):
            core = lax.axis_index("core")
            chip = lax.axis_index("inner")
            slot = lax.rem(chip, local)
            home = (core == lax.div(chip, local)).astype(jnp.int32)
            place = jnp.stack([core, slot, home])
            by_head = rates.transpose(0, 2, 1)
            packed = pack_rated(0, memory_keys, memory_values, by_head)
            got = exchange(packed)
            sent = [
                permute(
                    lax.dynamic_index_in_dim(one, slot, 0, False),
                    lambda o, i, p, c: (o, i, p, i // local) if c != i // local else None,
                )
                for one in fast
            ]
            state, own, rest = start_state(place, sent, fast)
            packed = pack_spans(queries, heads)
            got_queries = exchange(packed)
            outputs = None
            final = [None] * 3
            for span in range(spans):
                last = span + 1 == spans
                keep, give = gradients(place, own, rest, got)
                for matrix in ORDER:
                    received = other_core(give[matrix])
                    partial = combine(keep[matrix], received)
                    theirs = across(partial)
                    state[matrix], own[matrix] = update(state[matrix], partial, theirs)
                    rest[matrix] = other_core(own[matrix])
                    if last:
                        full = joined(place, own[matrix], rest[matrix])
                        near = [nearest(full, n) for n in range(1, local)]
                        along = matrix != ORDER[-1]
                        far = [
                            onward(near[0] if along else near[n - 1], n, along)
                            for n in range(1, local)
                        ]
                        final[matrix] = final_state(place, full, near, far)
                if not last:
                    packed = pack_rated(span + 1, memory_keys, memory_values, by_head)
                    got = exchange(packed)
                out = applied(place, own, rest, got_queries, span, spans)
                moved = exchange(out)
                outputs = unpack(moved, span, spans, outputs)
            return (outputs, *final)

        by_token = P(None, AXES, None)
        by_slot = P(("pair", "core"), None, None)
        return jax.shard_map(
            on_device,
            mesh=fine,
            in_specs=(by_token,) * 4 + (by_slot,) * 3,
            out_specs=(by_token,) + (by_slot,) * 3,
            check_vma=False,
        )(queries, memory_keys, memory_values, rates, fast_gate, fast_up, fast_down)

    return whole
```
